32 devices in a mesh: gx: 8 (over z, y), gy: 2 (over core), gz: 2 (over x).
Axes of the slice: x: 2, y: 2, z: 4, core: 2. Of those that a mesh axis runs over, the one named last changes fastest.
Arguments:
- populations: float32 [39, 24, 8, 256], P(None, 'gx', 'gy', 'gz'), may hold values from 0.5 to 1.5
- pore_mask: int32 [24, 8, 256], P('gx', 'gy', 'gz'), may hold values 0 or 1
Outputs:
- advanced: float32 [39, 24, 8, 256], P(None, 'gx', 'gy', 'gz')
The draws below stay inside these ranges and needn't reach their ends.
All inputs are finite; a program needn't handle non-finite values. No bound on the sum of `pore_mask` on one device may be relied on, other than what follows from the above.
Results may differ from the reference program's by a relative error of at most 0.0003.
Values sent between devices are 32-bit elements; how exact they have to be, the bound alone decides.
A program may use at most 64 MiB of HBM per device.

```python
import jax
import jax.numpy as jnp
from jax import lax

VELOCITIES = 39
STEPS = 1
NX = 24
NY = 8
NZ = 256


def touch_ends(result, own_key, smallest, top_value):
    longest = result.shape.index(max(result.shape))
    spots = []
    for shift in (0, 1):
        where = [jax.random.randint(jax.random.fold_in(own_key, axis), (), 0, length) for axis, length in enumerate(result.shape)]
        where[longest] = (where[longest] + shift) % result.shape[longest]
        spots.append(tuple(where))
    return result.at[spots[0]].set(smallest).at[spots[1]].set(top_value)


def block_levels(own_key, extent, cuts, smallest, high):
    def one(axis_at, parts):
        steps = jax.random.uniform(jax.random.fold_in(jax.random.fold_in(own_key, 6), axis_at), (parts,), jnp.float32, smallest / len(cuts), high / len(cuts))
        return jnp.repeat(jnp.exp(steps), extent[axis_at] // parts).reshape((-1,) + (1,) * (len(extent) - axis_at - 1))

    loudness = one(*cuts[0])
    for cut in cuts[1:]:
        loudness = loudness * one(*cut)
    return loudness


def setup_inputs(seed: int = 0) -> dict:
    streams_of = jax.random.split(jax.random.key(seed), 3)
    return {
        "populations": jnp.clip(0.5 + 1.0 * jax.random.uniform(streams_of[0], (VELOCITIES, NX, NY, NZ), jnp.float32) ** block_levels(streams_of[0], (VELOCITIES, NX, NY, NZ), ((1, 8), (2, 2), (3, 2)), -0.2, 0.2), 0.5, 1.5),
        "pore_mask": touch_ends((jax.random.randint(streams_of[1], (NX, NY, NZ), 0, 10) < 7).astype(jnp.int32), jax.random.fold_in(streams_of[1], 1), 0, 1),
    }


sound_sq = 2.0 / 3.0
relax_time = 0.8
pair_list = [(0, 0), (1, 1), (2, 2), (0, 1), (0, 2), (1, 2)]
triple_list = [(0, 0, 0), (1, 1, 1), (2, 2, 2), (0, 0, 1), (0, 0, 2), (1, 1, 0), (1, 1, 2), (2, 2, 0), (2, 2, 1), (0, 1, 2)]


def lattice_tables():
    shell_weights = {(0, 0, 0): 1.0 / 12.0, (0, 0, 1): 1.0 / 12.0, (1, 1, 1): 1.0 / 27.0, (0, 0, 2): 2.0 / 135.0, (0, 2, 2): 1.0 / 432.0, (0, 0, 3): 1.0 / 1620.0}
    speed_list = []
    weight_list = []
    for a in range(-3, 4):
        for b in range(-3, 4):
            for c in range(-3, 4):
                pattern = tuple(sorted((abs(a), abs(b), abs(c))))
                if pattern in shell_weights:
                    speed_list.append((a, b, c))
                    weight_list.append(shell_weights[pattern])
    count = len(speed_list)
    opposite = [speed_list.index((-v[0], -v[1], -v[2])) for v in speed_list]
    hermite = [[1.0] * count]
    scaling = [1.0]
    for a in range(3):
        hermite.append([float(v[a]) for v in speed_list])
        scaling.append(1.0 / sound_sq)
    for a, b in pair_list:
        hermite.append([float(v[a] * v[b]) - sound_sq * float(a == b) for v in speed_list])
        scaling.append((1.0 if a == b else 2.0) / (2.0 * sound_sq ** 2))
    for a, b, c in triple_list:
        hermite.append([float(v[a] * v[b] * v[c]) - sound_sq * (v[a] * float(b == c) + v[b] * float(a == c) + v[c] * float(a == b)) for v in speed_list])
        distinct = len(set((a, b, c)))
        scaling.append({1: 1.0, 2: 3.0, 3: 6.0}[distinct] / (6.0 * sound_sq ** 3))
    moment_count = len(hermite)
    project = [[hermite[j][k] * weight_list[k] for k in range(count)] for j in range(moment_count)]
    gram_matrix = [[sum(project[i][k] * hermite[j][k] for k in range(count)) for j in range(moment_count)] for i in range(moment_count)]
    hermite_t = [[hermite[j][k] for j in range(moment_count)] for k in range(count)]
    relaxing = [(1.0 - 1.0 / relax_time) * scaling[j] if j >= 4 else 0.0 for j in range(moment_count)]
    return (jnp.asarray(hermite_t, dtype=jnp.float32), jnp.asarray(project, dtype=jnp.float32), jnp.asarray(gram_matrix, dtype=jnp.float32),
            jnp.asarray(scaling, dtype=jnp.float32), jnp.asarray(relaxing, dtype=jnp.float32), speed_list, opposite)


def collide(state, pore_mask, tables):
    hermite_t, project, gram_matrix, scaling, relaxing, speeds, opposite = tables
    pop_count = state.shape[0]
    columns = state.reshape(pop_count, -1)
    moments = jnp.dot(project, columns, precision=lax.Precision.HIGHEST)
    density = moments[0]
    velocity = [moments[1 + a] / density for a in range(3)]
    pieces_list = [density] + [density * velocity[a] for a in range(3)]
    pieces_list = pieces_list + [density * velocity[a] * velocity[b] for a, b in pair_list]
    pieces_list = pieces_list + [density * velocity[a] * velocity[b] * velocity[c] for a, b, c in triple_list]
    equilibrium = scaling[:, None] * jnp.stack(pieces_list)
    excess = moments - jnp.dot(gram_matrix, equilibrium, precision=lax.Precision.HIGHEST)
    coeffs = equilibrium + relaxing[:, None] * excess
    collided = jnp.dot(hermite_t, coeffs, precision=lax.Precision.HIGHEST)
    mirrored = jnp.stack([columns[opposite[k]] for k in range(pop_count)])
    return jnp.where(pore_mask.reshape(1, -1) == 1, collided, mirrored).reshape(state.shape)


def reference(populations, pore_mask):
    tables = lattice_tables()
    speeds = tables[5]

    def collide_plane(operands):
        return collide(operands[0], operands[1], tables)

    state = populations
    for repeat in range(STEPS):
        planes = jnp.moveaxis(state, 1, 0)
        collided = lax.map(collide_plane, (planes, pore_mask))
        shifted = [jnp.roll(collided[:, k], (speeds[k][0], speeds[k][1], speeds[k][2]), axis=(0, 1, 2)) for k in range(len(speeds))]
        state = jnp.stack(shifted)
    return state
```

```python
import functools

import jax
import jax.numpy as jnp
from jax import lax
from jax.experimental import pallas as pl
from jax.experimental.pallas import tpu as pltpu
from jax.sharding import PartitionSpec as P

MESH = pl.DeviceIdType.MESH

sound_sq = 2.0 / 3.0
relax_time = 0.8
pair_list = [(0, 0), (1, 1), (2, 2), (0, 1), (0, 2), (1, 2)]
triple_list = [
    (0, 0, 0),
    (1, 1, 1),
    (2, 2, 2),
    (0, 0, 1),
    (0, 0, 2),
    (1, 1, 0),
    (1, 1, 2),
    (2, 2, 0),
    (2, 2, 1),
    (0, 1, 2),
]
shell_weights = {
    (0, 0, 0): 1.0 / 12.0,
    (0, 0, 1): 1.0 / 12.0,
    (1, 1, 1): 1.0 / 27.0,
    (0, 0, 2): 2.0 / 135.0,
    (0, 2, 2): 1.0 / 432.0,
    (0, 0, 3): 1.0 / 1620.0,
}


def lattice():
    speeds = []
    weights = []
    for a in range(-3, 4):
        for b in range(-3, 4):
            for c in range(-3, 4):
                pattern = tuple(sorted((abs(a), abs(b), abs(c))))
                if pattern in shell_weights:
                    speeds.append((a, b, c))
                    weights.append(shell_weights[pattern])
    return speeds, weights


speeds, weights = lattice()
opposite = [speeds.index((-v[0], -v[1], -v[2])) for v in speeds]


def accumulate(total, factor, term):
    if factor == 0:
        return total
    if total is None:
        return term if factor == 1 else factor * term
    if factor == 1:
        return total + term
    if factor == -1:
        return total - term
    return total + factor * term


def collide(load, pore):
    rest = speeds.index((0, 0, 0))
    pairs = [(k, opposite[k]) for k in range(len(speeds)) if k > opposite[k]]
    density = weights[rest] * load(rest)
    first = [None] * 3
    second = {ab: None for ab in pair_list}
    third = {abc: None for abc in triple_list}
    for shell in shell_weights:
        members = [(k, o) for k, o in pairs if tuple(sorted(map(abs, speeds[k]))) == shell]
        if not members:
            continue
        part0, part1 = None, [None] * 3
        part2 = {ab: None for ab in pair_list}
        part3 = {abc: None for abc in triple_list}
        for k, o in members:
            v = speeds[k]
            even = load(k) + load(o)
            odd = load(k) - load(o)
            part0 = accumulate(part0, 1, even)
            for a, b in pair_list:
                part2[a, b] = accumulate(part2[a, b], v[a] * v[b], even)
            for a in range(3):
                part1[a] = accumulate(part1[a], v[a], odd)
            for a, b, c in triple_list:
                part3[a, b, c] = accumulate(part3[a, b, c], v[a] * v[b] * v[c], odd)
        w = shell_weights[shell]
        density = accumulate(density, w, part0)
        for a in range(3):
            first[a] = accumulate(first[a], w, part1[a])
        for ab in pair_list:
            if part2[ab] is not None:
                second[ab] = accumulate(second[ab], w, part2[ab])
        for abc in triple_list:
            if part3[abc] is not None:
                third[abc] = accumulate(third[abc], w, part3[abc])

    u = [first[a] / density for a in range(3)]
    relax = 1.0 - 1.0 / relax_time
    const = density
    linear = [first[a] * (1.0 / sound_sq) for a in range(3)]
    quad, cubic = {}, {}
    flux = {}
    for a, b in pair_list:
        flux[a, b] = first[a] * u[b]
        moment = second[a, b]
        if a == b:
            moment = moment - sound_sq * density
        scale = (1.0 if a == b else 2.0) / (2.0 * sound_sq**2)
        quad[a, b] = (scale * (1.0 - relax)) * flux[a, b] + (scale * relax) * moment
        if a == b:
            const = const - sound_sq * quad[a, b]
    for a, b, c in triple_list:
        moment = third[a, b, c]
        if a == b == c:
            moment = moment - (3.0 * sound_sq) * first[a]
        elif a == b:
            moment = moment - sound_sq * first[c]
        pair = (a, b) if (a, b) in flux else (b, a)
        scale = {1: 1.0, 2: 3.0, 3: 6.0}[len({a, b, c})] / (6.0 * sound_sq**3)
        cubic[a, b, c] = (scale * (1.0 - relax)) * (flux[pair] * u[c]) + (scale * relax) * moment
        if a == b == c:
            linear[a] = linear[a] - (3.0 * sound_sq) * cubic[a, b, c]
        elif a == b:
            linear[c] = linear[c] - sound_sq * cubic[a, b, c]

    yield rest, jnp.where(pore, const, load(rest))
    for k, o in pairs:
        v = speeds[k]
        even, odd = const, None
        for a, b in pair_list:
            even = accumulate(even, float(v[a] * v[b]), quad[a, b])
        for a in range(3):
            odd = accumulate(odd, float(v[a]), linear[a])
        for a, b, c in triple_list:
            odd = accumulate(odd, float(v[a] * v[b] * v[c]), cubic[a, b, c])
        yield k, jnp.where(pore, even + odd, load(o))
        yield o, jnp.where(pore, even - odd, load(k))


def cut(speed, extent):
    if speed >= 0:
        return (0, extent - speed), (speed, extent), (extent - speed, extent), (0, speed)
    return (-speed, extent), (0, extent + speed), (0, -speed), (extent + speed, extent)


def merge_key(speed, extent):
    return abs(speed) if 2 * abs(speed) <= extent else speed


def make_plan(nx, ny):
    sizes, slots, pieces = {}, {}, []
    for k, (cx, cy, cz) in enumerate(speeds):
        stay_from, stay_to, leave_from, leave_to = cut(cx, nx)
        own = []
        for source, land, dx in ((stay_from, stay_to, 0), (leave_from, leave_to, (cx > 0) - (cx < 0))):
            count = source[1] - source[0]
            if count == 0:
                continue
            where = {}
            for oy in (0, 1):
                for oz in (0, 1):
                    if (oy and not cy) or (oz and not cz) or (dx, oy, oz) == (0, 0, 0):
                        continue
                    key = (
                        dx,
                        oy,
                        oz,
                        cx,
                        merge_key(cy, ny) if oy else (cy,),
                        abs(cz) if oz else (cz,),
                    )
                    if key not in slots:
                        slots[key] = sizes.get((dx, oy, oz), 0)
                        sizes[dx, oy, oz] = slots[key] + count
                    where[oy, oz] = slots[key]
            own.append((source, land, dx, where))
        pieces.append(own)
    return sizes, pieces


def neighbours(count):
    return (1,) if count == 2 else (1, -1)


def step_kernel(counts, sizes, pieces, messages, names, pop_ref, mask_ref, out_ref, *scratch):
    nx, ny, nz = out_ref.shape[1:]
    send = dict(zip(names, scratch[: len(names)]))
    recv = dict(zip(messages, scratch[len(names) : len(names) + len(messages)]))
    send_sem, recv_sem = scratch[len(names) + len(messages) :]
    here = [lax.axis_index(axis) for axis in ("gx", "gy", "gz")]

    def target(step):
        return {
            axis: lax.rem(at + (s + count), count)
            for axis, at, s, count in zip(("gx", "gy", "gz"), here, step, counts)
            if s
        }

    barrier = pltpu.get_barrier_semaphore()
    for step in messages:
        pl.semaphore_signal(barrier, inc=1, device_id=target(step), device_id_type=MESH)

    def block(span, rows, lanes):
        return (slice(*span), slice(*rows), slice(*lanes))

    pore = mask_ref[...] == 1
    every_lane = (0, nz)
    for k, plane in collide(lambda j: pop_ref[j], pore):
        cx, cy, cz = speeds[k]
        if cz:
            plane = pltpu.roll(plane, cz % nz, 2)
        y_stay, y_land, y_leave, y_wrap = cut(cy, ny)
        z_wrap = cut(cz, nz)[3]
        for source, land, dx, where in pieces[k]:
            count = source[1] - source[0]
            value = plane[slice(*source)]
            kept = value[:, slice(*y_stay)]
            if dx == 0:
                out_ref[(k,) + block(land, y_land, every_lane)] = kept
            else:
                at = where[0, 0]
                send[dx, 0, 0][block((at, at + count), y_land, every_lane)] = kept
            if cy:
                at = where[1, 0]
                moved = value[:, slice(*y_leave)]
                send[dx, 1, 0][block((at, at + count), y_wrap, every_lane)] = moved
            if cz:
                at = where[0, 1]
                send[dx, 0, 1][block((at, at + count), y_land, z_wrap)] = kept[:, :, slice(*z_wrap)]
            if cy and cz:
                at = where[1, 1]
                send[dx, 1, 1][block((at, at + count), y_wrap, z_wrap)] = moved[:, :, slice(*z_wrap)]

    pl.semaphore_wait(barrier, len(messages))
    copies = {}
    for number, step in enumerate(messages):
        kind = (step[0], abs(step[1]), abs(step[2]))
        copies[step] = pltpu.make_async_remote_copy(
            src_ref=send[kind],
            dst_ref=recv[step],
            send_sem=send_sem.at[number],
            recv_sem=recv_sem.at[number],
            device_id=target(step),
            device_id_type=MESH,
        )
        copies[step].start()

    def came_by(step, speed):
        return step == 0 or step * speed > 0

    for step in reversed(messages):
        copies[step].wait_recv()
        got = recv[step]
        dx, sy, sz = step
        for k, (cx, cy, cz) in enumerate(speeds):
            if (sy and not cy) or (sz and not cz):
                continue
            if counts[1] != 2 and not came_by(sy, cy):
                continue
            if counts[2] != 2 and not came_by(sz, cz):
                continue
            _, y_land, _, y_wrap = cut(cy, ny)
            rows = y_wrap if sy else y_land
            lanes = cut(cz, nz)[3] if sz else every_lane
            for source, land, piece_dx, where in pieces[k]:
                if piece_dx != dx:
                    continue
                at = where[abs(sy), abs(sz)]
                span = (at, at + source[1] - source[0])
                out_ref[(k,) + block(land, rows, lanes)] = got[block(span, rows, lanes)]
    for step in messages:
        copies[step].wait_send()


def body(counts, populations, pore_mask):
    nx, ny, nz = populations.shape[1:]
    sizes, pieces = make_plan(nx, ny)
    names = sorted(sizes)
    messages = []
    for dx, oy, oz in [(dx, oy, oz) for oz in (1, 0) for oy in (1, 0) for dx in (1, -1)] + [
        (0, 1, 1),
        (0, 0, 1),
        (0, 1, 0),
    ]:
        for sy in neighbours(counts[1]) if oy else (0,):
            for sz in neighbours(counts[2]) if oz else (0,):
                messages.append((dx, sy, sz))
    kernel = functools.partial(step_kernel, counts, sizes, pieces, messages, names)
    shape = lambda name: pltpu.VMEM((sizes[name[0], abs(name[1]), abs(name[2])], ny, nz), jnp.float32)
    return pl.pallas_call(
        kernel,
        out_shape=jax.ShapeDtypeStruct(populations.shape, populations.dtype),
        in_specs=[pl.BlockSpec(memory_space=pltpu.VMEM)] * 2,
        out_specs=pl.BlockSpec(memory_space=pltpu.VMEM),
        scratch_shapes=[shape(name) for name in names]
        + [shape(step) for step in messages]
        + [pltpu.SemaphoreType.DMA((len(messages),)), pltpu.SemaphoreType.DMA((len(messages),))],
        compiler_params=pltpu.CompilerParams(collective_id=0, has_side_effects=True),
    )(populations, pore_mask)


def solution(mesh):
    counts = tuple(mesh.shape[axis] for axis in ("gx", "gy", "gz"))
    placed = (P(None, "gx", "gy", "gz"), P("gx", "gy", "gz"))
    return jax.shard_map(
        functools.partial(body, counts),
        mesh=mesh,
        in_specs=placed,
        out_specs=P(None, "gx", "gy", "gz"),
        check_vma=False,
    )
```

```python
import functools

import jax
import jax.numpy as jnp
from jax import lax
from jax.experimental import pallas as pl
from jax.experimental.pallas import tpu as pltpu
from jax.sharding import PartitionSpec as P

MESH = pl.DeviceIdType.MESH

sound_sq = 2.0 / 3.0
relax_time = 0.8
pair_list = [(0, 0), (1, 1), (2, 2), (0, 1), (0, 2), (1, 2)]
triple_list = [
    (0, 0, 0),
    (1, 1, 1),
    (2, 2, 2),
    (0, 0, 1),
    (0, 0, 2),
    (1, 1, 0),
    (1, 1, 2),
    (2, 2, 0),
    (2, 2, 1),
    (0, 1, 2),
]
shell_weights = {
    (0, 0, 0): 1.0 / 12.0,
    (0, 0, 1): 1.0 / 12.0,
    (1, 1, 1): 1.0 / 27.0,
    (0, 0, 2): 2.0 / 135.0,
    (0, 2, 2): 1.0 / 432.0,
    (0, 0, 3): 1.0 / 1620.0,
}


def lattice():
    speeds = []
    weights = []
    for a in range(-3, 4):
        for b in range(-3, 4):
            for c in range(-3, 4):
                pattern = tuple(sorted((abs(a), abs(b), abs(c))))
                if pattern in shell_weights:
                    speeds.append((a, b, c))
                    weights.append(shell_weights[pattern])
    return speeds, weights


speeds, weights = lattice()
opposite = [speeds.index((-v[0], -v[1], -v[2])) for v in speeds]


def accumulate(total, factor, term):
    if factor == 0:
        return total
    if total is None:
        return term if factor == 1 else factor * term
    if factor == 1:
        return total + term
    if factor == -1:
        return total - term
    return total + factor * term


def collide(load, pore):
    rest = speeds.index((0, 0, 0))
    pairs = [(k, opposite[k]) for k in range(len(speeds)) if k > opposite[k]]
    density = weights[rest] * load(rest)
    first = [None] * 3
    second = {ab: None for ab in pair_list}
    third = {abc: None for abc in triple_list}
    for shell in shell_weights:
        members = [(k, o) for k, o in pairs if tuple(sorted(map(abs, speeds[k]))) == shell]
        if not members:
            continue
        part0, part1 = None, [None] * 3
        part2 = {ab: None for ab in pair_list}
        part3 = {abc: None for abc in triple_list}
        for k, o in members:
            v = speeds[k]
            even = load(k) + load(o)
            odd = load(k) - load(o)
            part0 = accumulate(part0, 1, even)
            for a, b in pair_list:
                part2[a, b] = accumulate(part2[a, b], v[a] * v[b], even)
            for a in range(3):
                part1[a] = accumulate(part1[a], v[a], odd)
            for a, b, c in triple_list:
                part3[a, b, c] = accumulate(part3[a, b, c], v[a] * v[b] * v[c], odd)
        w = shell_weights[shell]
        density = accumulate(density, w, part0)
        for a in range(3):
            first[a] = accumulate(first[a], w, part1[a])
        for ab in pair_list:
            if part2[ab] is not None:
                second[ab] = accumulate(second[ab], w, part2[ab])
        for abc in triple_list:
            if part3[abc] is not None:
                third[abc] = accumulate(third[abc], w, part3[abc])

    u = [first[a] / density for a in range(3)]
    relax = 1.0 - 1.0 / relax_time
    const = density
    linear = [first[a] * (1.0 / sound_sq) for a in range(3)]
    quad, cubic = {}, {}
    flux = {}
    for a, b in pair_list:
        flux[a, b] = first[a] * u[b]
        moment = second[a, b]
        if a == b:
            moment = moment - sound_sq * density
        scale = (1.0 if a == b else 2.0) / (2.0 * sound_sq**2)
        quad[a, b] = (scale * (1.0 - relax)) * flux[a, b] + (scale * relax) * moment
        if a == b:
            const = const - sound_sq * quad[a, b]
    for a, b, c in triple_list:
        moment = third[a, b, c]
        if a == b == c:
            moment = moment - (3.0 * sound_sq) * first[a]
        elif a == b:
            moment = moment - sound_sq * first[c]
        pair = (a, b) if (a, b) in flux else (b, a)
        scale = {1: 1.0, 2: 3.0, 3: 6.0}[len({a, b, c})] / (6.0 * sound_sq**3)
        cubic[a, b, c] = (scale * (1.0 - relax)) * (flux[pair] * u[c]) + (scale * relax) * moment
        if a == b == c:
            linear[a] = linear[a] - (3.0 * sound_sq) * cubic[a, b, c]
        elif a == b:
            linear[c] = linear[c] - sound_sq * cubic[a, b, c]

    yield rest, jnp.where(pore, const, load(rest))
    for k, o in pairs:
        v = speeds[k]
        even, odd = const, None
        for a, b in pair_list:
            even = accumulate(even, float(v[a] * v[b]), quad[a, b])
        for a in range(3):
            odd = accumulate(odd, float(v[a]), linear[a])
        for a, b, c in triple_list:
            odd = accumulate(odd, float(v[a] * v[b] * v[c]), cubic[a, b, c])
        yield k, jnp.where(pore, even + odd, load(o))
        yield o, jnp.where(pore, even - odd, load(k))


def cut(speed, extent):
    if speed >= 0:
        return (0, extent - speed), (speed, extent), (extent - speed, extent), (0, speed)
    return (-speed, extent), (0, extent + speed), (0, -speed), (extent + speed, extent)


def merge_key(speed, extent):
    return abs(speed) if 2 * abs(speed) <= extent else speed


def make_plan(nx, ny):
    sizes, slots, pieces = {}, {}, []
    for k, (cx, cy, cz) in enumerate(speeds):
        stay_from, stay_to, leave_from, leave_to = cut(cx, nx)
        own = []
        for source, land, dx in ((stay_from, stay_to, 0), (leave_from, leave_to, (cx > 0) - (cx < 0))):
            count = source[1] - source[0]
            if count == 0:
                continue
            where = {}
            for oy in (0, 1):
                for oz in (0, 1):
                    if (oy and not cy) or (oz and not cz) or (dx, oy, oz) == (0, 0, 0):
                        continue
                    key = (
                        dx,
                        oy,
                        oz,
                        cx,
                        merge_key(cy, ny) if oy else (cy,),
                        abs(cz) if oz else (cz,),
                    )
                    if key not in slots:
                        slots[key] = sizes.get((dx, oy, oz), 0)
                        sizes[dx, oy, oz] = slots[key] + count
                    where[oy, oz] = slots[key]
            own.append((source, land, dx, where))
        pieces.append(own)
    return sizes, pieces


def neighbours(count):
    return (1,) if count == 2 else (1, -1)


def step_kernel(counts, sizes, pieces, messages, names, pop_hbm, mask_hbm, out_ref, *scratch):
    nx, ny, nz = out_ref.shape[1:]
    *scratch, pop_ref, mask_ref, load_sem = scratch
    send = dict(zip(names, scratch[: len(names)]))
    recv = dict(zip(messages, scratch[len(names) : len(names) + len(messages)]))
    send_sem, recv_sem = scratch[len(names) + len(messages) :]
    here = [lax.axis_index(axis) for axis in ("gx", "gy", "gz")]

    def target(step):
        return {
            axis: lax.rem(at + (s + count), count)
            for axis, at, s, count in zip(("gx", "gy", "gz"), here, step, counts)
            if s
        }

    barrier = pltpu.get_barrier_semaphore()
    for step in messages:
        pl.semaphore_signal(barrier, inc=1, device_id=target(step), device_id_type=MESH)

    loads = [
        pltpu.make_async_copy(pop_hbm, pop_ref, load_sem.at[0]),
        pltpu.make_async_copy(mask_hbm, mask_ref, load_sem.at[1]),
    ]
    for load in loads:
        load.start()
    for load in loads:
        load.wait()

    def block(span, rows, lanes):
        return (slice(*span), slice(*rows), slice(*lanes))

    pore = mask_ref[...] == 1
    every_lane = (0, nz)
    for k, plane in collide(lambda j: pop_ref[j], pore):
        cx, cy, cz = speeds[k]
        if cz:
            plane = pltpu.roll(plane, cz % nz, 2)
        y_stay, y_land, y_leave, y_wrap = cut(cy, ny)
        z_wrap = cut(cz, nz)[3]
        for source, land, dx, where in pieces[k]:
            count = source[1] - source[0]
            value = plane[slice(*source)]
            kept = value[:, slice(*y_stay)]
            if dx == 0:
                out_ref[(k,) + block(land, y_land, every_lane)] = kept
            else:
                at = where[0, 0]
                send[dx, 0, 0][block((at, at + count), y_land, every_lane)] = kept
            if cy:
                at = where[1, 0]
                moved = value[:, slice(*y_leave)]
                send[dx, 1, 0][block((at, at + count), y_wrap, every_lane)] = moved
            if cz:
                at = where[0, 1]
                send[dx, 0, 1][block((at, at + count), y_land, z_wrap)] = kept[:, :, slice(*z_wrap)]
            if cy and cz:
                at = where[1, 1]
                send[dx, 1, 1][block((at, at + count), y_wrap, z_wrap)] = moved[:, :, slice(*z_wrap)]

    pl.semaphore_wait(barrier, len(messages))
    copies = {}
    for number, step in enumerate(messages):
        kind = (step[0], abs(step[1]), abs(step[2]))
        copies[step] = pltpu.make_async_remote_copy(
            src_ref=send[kind],
            dst_ref=recv[step],
            send_sem=send_sem.at[number],
            recv_sem=recv_sem.at[number],
            device_id=target(step),
            device_id_type=MESH,
        )
        copies[step].start()

    def came_by(step, speed):
        return step == 0 or step * speed > 0

    for step in reversed(messages):
        copies[step].wait_recv()
        got = recv[step]
        dx, sy, sz = step
        for k, (cx, cy, cz) in enumerate(speeds):
            if (sy and not cy) or (sz and not cz):
                continue
            if counts[1] != 2 and not came_by(sy, cy):
                continue
            if counts[2] != 2 and not came_by(sz, cz):
                continue
            _, y_land, _, y_wrap = cut(cy, ny)
            rows = y_wrap if sy else y_land
            lanes = cut(cz, nz)[3] if sz else every_lane
            for source, land, piece_dx, where in pieces[k]:
                if piece_dx != dx:
                    continue
                at = where[abs(sy), abs(sz)]
                span = (at, at + source[1] - source[0])
                out_ref[(k,) + block(land, rows, lanes)] = got[block(span, rows, lanes)]
    for step in messages:
        copies[step].wait_send()


def body(counts, populations, pore_mask):
    nx, ny, nz = populations.shape[1:]
    sizes, pieces = make_plan(nx, ny)
    names = sorted(sizes)
    messages = []
    for dx, oy, oz in [(dx, oy, oz) for oz in (1, 0) for oy in (1, 0) for dx in (1, -1)] + [
        (0, 1, 1),
        (0, 0, 1),
        (0, 1, 0),
    ]:
        for sy in neighbours(counts[1]) if oy else (0,):
            for sz in neighbours(counts[2]) if oz else (0,):
                messages.append((dx, sy, sz))
    kernel = functools.partial(step_kernel, counts, sizes, pieces, messages, names)
    shape = lambda name: pltpu.VMEM((sizes[name[0], abs(name[1]), abs(name[2])], ny, nz), jnp.float32)
    return pl.pallas_call(
        kernel,
        out_shape=pltpu.VMEM(populations.shape, populations.dtype),
        in_specs=[pl.BlockSpec(memory_space=pl.ANY)] * 2,
        out_specs=pl.BlockSpec(memory_space=pltpu.VMEM),
        scratch_shapes=[shape(name) for name in names]
        + [shape(step) for step in messages]
        + [pltpu.SemaphoreType.DMA((len(messages),)), pltpu.SemaphoreType.DMA((len(messages),))]
        + [
            pltpu.VMEM(populations.shape, populations.dtype),
            pltpu.VMEM(pore_mask.shape, pore_mask.dtype),
            pltpu.SemaphoreType.DMA((2,)),
        ],
        compiler_params=pltpu.CompilerParams(collective_id=0, has_side_effects=True),
    )(populations, pore_mask)


def solution(mesh):
    counts = tuple(mesh.shape[axis] for axis in ("gx", "gy", "gz"))
    placed = (P(None, "gx", "gy", "gz"), P("gx", "gy", "gz"))
    return jax.shard_map(
        functools.partial(body, counts),
        mesh=mesh,
        in_specs=placed,
        out_specs=P(None, "gx", "gy", "gz"),
        check_vma=False,
    )
```

```python
import functools

import jax
import jax.numpy as jnp
from jax import lax
from jax.experimental import pallas as pl
from jax.experimental.pallas import tpu as pltpu
from jax.sharding import PartitionSpec as P

MESH = pl.DeviceIdType.MESH

sound_sq = 2.0 / 3.0
relax_time = 0.8
pair_list = [(0, 0), (1, 1), (2, 2), (0, 1), (0, 2), (1, 2)]
triple_list = [
    (0, 0, 0),
    (1, 1, 1),
    (2, 2, 2),
    (0, 0, 1),
    (0, 0, 2),
    (1, 1, 0),
    (1, 1, 2),
    (2, 2, 0),
    (2, 2, 1),
    (0, 1, 2),
]
shell_weights = {
    (0, 0, 0): 1.0 / 12.0,
    (0, 0, 1): 1.0 / 12.0,
    (1, 1, 1): 1.0 / 27.0,
    (0, 0, 2): 2.0 / 135.0,
    (0, 2, 2): 1.0 / 432.0,
    (0, 0, 3): 1.0 / 1620.0,
}


def lattice():
    speeds = []
    weights = []
    for a in range(-3, 4):
        for b in range(-3, 4):
            for c in range(-3, 4):
                pattern = tuple(sorted((abs(a), abs(b), abs(c))))
                if pattern in shell_weights:
                    speeds.append((a, b, c))
                    weights.append(shell_weights[pattern])
    return speeds, weights


speeds, weights = lattice()
opposite = [speeds.index((-v[0], -v[1], -v[2])) for v in speeds]


def accumulate(total, factor, term):
    if factor == 0:
        return total
    if total is None:
        return term if factor == 1 else factor * term
    if factor == 1:
        return total + term
    if factor == -1:
        return total - term
    return total + factor * term


def collide(load, pore):
    rest = speeds.index((0, 0, 0))
    pairs = [(k, opposite[k]) for k in range(len(speeds)) if k > opposite[k]]
    density = weights[rest] * load(rest)
    first = [None] * 3
    second = {ab: None for ab in pair_list}
    third = {abc: None for abc in triple_list}
    for shell in shell_weights:
        members = [(k, o) for k, o in pairs if tuple(sorted(map(abs, speeds[k]))) == shell]
        if not members:
            continue
        part0, part1 = None, [None] * 3
        part2 = {ab: None for ab in pair_list}
        part3 = {abc: None for abc in triple_list}
        for k, o in members:
            v = speeds[k]
            even = load(k) + load(o)
            odd = load(k) - load(o)
            part0 = accumulate(part0, 1, even)
            for a, b in pair_list:
                part2[a, b] = accumulate(part2[a, b], v[a] * v[b], even)
            for a in range(3):
                part1[a] = accumulate(part1[a], v[a], odd)
            for a, b, c in triple_list:
                part3[a, b, c] = accumulate(part3[a, b, c], v[a] * v[b] * v[c], odd)
        w = shell_weights[shell]
        density = accumulate(density, w, part0)
        for a in range(3):
            first[a] = accumulate(first[a], w, part1[a])
        for ab in pair_list:
            if part2[ab] is not None:
                second[ab] = accumulate(second[ab], w, part2[ab])
        for abc in triple_list:
            if part3[abc] is not None:
                third[abc] = accumulate(third[abc], w, part3[abc])

    u = [first[a] / density for a in range(3)]
    relax = 1.0 - 1.0 / relax_time
    const = density
    linear = [first[a] * (1.0 / sound_sq) for a in range(3)]
    quad, cubic = {}, {}
    flux = {}
    for a, b in pair_list:
        flux[a, b] = first[a] * u[b]
        moment = second[a, b]
        if a == b:
            moment = moment - sound_sq * density
        scale = (1.0 if a == b else 2.0) / (2.0 * sound_sq**2)
        quad[a, b] = (scale * (1.0 - relax)) * flux[a, b] + (scale * relax) * moment
        if a == b:
            const = const - sound_sq * quad[a, b]
    for a, b, c in triple_list:
        moment = third[a, b, c]
        if a == b == c:
            moment = moment - (3.0 * sound_sq) * first[a]
        elif a == b:
            moment = moment - sound_sq * first[c]
        pair = (a, b) if (a, b) in flux else (b, a)
        scale = {1: 1.0, 2: 3.0, 3: 6.0}[len({a, b, c})] / (6.0 * sound_sq**3)
        cubic[a, b, c] = (scale * (1.0 - relax)) * (flux[pair] * u[c]) + (scale * relax) * moment
        if a == b == c:
            linear[a] = linear[a] - (3.0 * sound_sq) * cubic[a, b, c]
        elif a == b:
            linear[c] = linear[c] - sound_sq * cubic[a, b, c]

    for k, o in sorted(pairs, key=lambda pair: speeds[pair[0]][0] == 0):
        v = speeds[k]
        even, odd = const, None
        for a, b in pair_list:
            even = accumulate(even, float(v[a] * v[b]), quad[a, b])
        for a in range(3):
            odd = accumulate(odd, float(v[a]), linear[a])
        for a, b, c in triple_list:
            odd = accumulate(odd, float(v[a] * v[b] * v[c]), cubic[a, b, c])
        yield k, jnp.where(pore, even + odd, load(o))
        yield o, jnp.where(pore, even - odd, load(k))
    yield rest, jnp.where(pore, const, load(rest))


def cut(speed, extent):
    if speed >= 0:
        return (0, extent - speed), (speed, extent), (extent - speed, extent), (0, speed)
    return (-speed, extent), (0, extent + speed), (0, -speed), (extent + speed, extent)


def merge_key(speed, extent):
    return abs(speed) if 2 * abs(speed) <= extent else speed


def make_plan(nx, ny):
    sizes, slots, pieces = {}, {}, []
    for k, (cx, cy, cz) in enumerate(speeds):
        stay_from, stay_to, leave_from, leave_to = cut(cx, nx)
        own = []
        for source, land, dx in ((stay_from, stay_to, 0), (leave_from, leave_to, (cx > 0) - (cx < 0))):
            count = source[1] - source[0]
            if count == 0:
                continue
            where = {}
            for oy in (0, 1):
                for oz in (0, 1):
                    if (oy and not cy) or (oz and not cz) or (dx, oy, oz) == (0, 0, 0):
                        continue
                    key = (
                        dx,
                        oy,
                        oz,
                        cx,
                        merge_key(cy, ny) if oy else (cy,),
                        abs(cz) if oz else (cz,),
                    )
                    if key not in slots:
                        slots[key] = sizes.get((dx, oy, oz), 0)
                        sizes[dx, oy, oz] = slots[key] + count
                    where[oy, oz] = slots[key]
            own.append((source, land, dx, where))
        pieces.append(own)
    return sizes, pieces


def neighbours(count):
    return (1,) if count == 2 else (1, -1)


def step_kernel(counts, sizes, pieces, messages, names, pop_hbm, mask_hbm, out_ref, *scratch):
    nx, ny, nz = out_ref.shape[1:]
    *scratch, pop_ref, mask_ref, load_sem = scratch
    send = dict(zip(names, scratch[: len(names)]))
    recv = dict(zip(messages, scratch[len(names) : len(names) + len(messages)]))
    send_sem, recv_sem, ready = scratch[len(names) + len(messages) :]
    here = [lax.axis_index(axis) for axis in ("gx", "gy", "gz")]

    def target(step):
        return {
            axis: lax.rem(at + (s + count), count)
            for axis, at, s, count in zip(("gx", "gy", "gz"), here, step, counts)
            if s
        }

    barrier = pltpu.get_barrier_semaphore()
    for step in messages:
        if step[0] <= 0:
            pl.semaphore_signal(barrier, inc=1, device_id=target(step), device_id_type=MESH)

    loads = [
        pltpu.make_async_copy(pop_hbm, pop_ref, load_sem.at[0]),
        pltpu.make_async_copy(mask_hbm, mask_ref, load_sem.at[1]),
    ]
    for load in loads:
        load.start()
    for load in loads:
        load.wait()

    def block(span, rows, lanes):
        return (slice(*span), slice(*rows), slice(*lanes))

    copies = {}
    for number, step in enumerate(messages):
        kind = (step[0], abs(step[1]), abs(step[2]))
        copies[step] = pltpu.make_async_remote_copy(
            src_ref=send[kind],
            dst_ref=recv[step],
            send_sem=send_sem.at[number],
            recv_sem=recv_sem.at[number],
            device_id=target(step),
            device_id_type=MESH,
        )
    above = sum(step[0] > 0 for step in messages)

    pore = mask_ref[...] == 1
    every_lane = (0, nz)
    moving = sum(speed[0] != 0 for speed in speeds)
    for done, (k, plane) in enumerate(collide(lambda j: pop_ref[j], pore)):
        if done == moving:
            pl.semaphore_wait(barrier, len(messages) - above)
            for step in messages:
                if step[0] > 0:
                    pl.semaphore_signal(ready, inc=1, device_id=target(step), device_id_type=MESH)
                    copies[step].start()
        cx, cy, cz = speeds[k]
        if cz:
            plane = pltpu.roll(plane, cz % nz, 2)
        y_stay, y_land, y_leave, y_wrap = cut(cy, ny)
        z_wrap = cut(cz, nz)[3]
        for source, land, dx, where in pieces[k]:
            count = source[1] - source[0]
            value = plane[slice(*source)]
            kept = value[:, slice(*y_stay)]
            if dx == 0:
                out_ref[(k,) + block(land, y_land, every_lane)] = kept
            else:
                at = where[0, 0]
                send[dx, 0, 0][block((at, at + count), y_land, every_lane)] = kept
            if cy:
                at = where[1, 0]
                moved = value[:, slice(*y_leave)]
                send[dx, 1, 0][block((at, at + count), y_wrap, every_lane)] = moved
            if cz:
                at = where[0, 1]
                send[dx, 0, 1][block((at, at + count), y_land, z_wrap)] = kept[:, :, slice(*z_wrap)]
            if cy and cz:
                at = where[1, 1]
                send[dx, 1, 1][block((at, at + count), y_wrap, z_wrap)] = moved[:, :, slice(*z_wrap)]

    for step in messages:
        if step[0] == 0:
            copies[step].start()
    pl.semaphore_wait(ready, above)
    for step in messages:
        if step[0] < 0:
            copies[step].start()

    def came_by(step, speed):
        return step == 0 or step * speed > 0

    for step in reversed(messages):
        copies[step].wait_recv()
        got = recv[step]
        dx, sy, sz = step
        for k, (cx, cy, cz) in enumerate(speeds):
            if (sy and not cy) or (sz and not cz):
                continue
            if counts[1] != 2 and not came_by(sy, cy):
                continue
            if counts[2] != 2 and not came_by(sz, cz):
                continue
            _, y_land, _, y_wrap = cut(cy, ny)
            rows = y_wrap if sy else y_land
            lanes = cut(cz, nz)[3] if sz else every_lane
            for source, land, piece_dx, where in pieces[k]:
                if piece_dx != dx:
                    continue
                at = where[abs(sy), abs(sz)]
                span = (at, at + source[1] - source[0])
                out_ref[(k,) + block(land, rows, lanes)] = got[block(span, rows, lanes)]
    for step in messages:
        copies[step].wait_send()


def body(counts, populations, pore_mask):
    nx, ny, nz = populations.shape[1:]
    sizes, pieces = make_plan(nx, ny)
    names = sorted(sizes)
    messages = []
    for dx, oy, oz in [(dx, oy, oz) for oz in (1, 0) for oy in (1, 0) for dx in (1, -1)] + [
        (0, 1, 1),
        (0, 0, 1),
        (0, 1, 0),
    ]:
        for sy in neighbours(counts[1]) if oy else (0,):
            for sz in neighbours(counts[2]) if oz else (0,):
                messages.append((dx, sy, sz))
    kernel = functools.partial(step_kernel, counts, sizes, pieces, messages, names)
    shape = lambda name: pltpu.VMEM((sizes[name[0], abs(name[1]), abs(name[2])], ny, nz), jnp.float32)
    return pl.pallas_call(
        kernel,
        out_shape=pltpu.VMEM(populations.shape, populations.dtype),
        in_specs=[pl.BlockSpec(memory_space=pl.ANY)] * 2,
        out_specs=pl.BlockSpec(memory_space=pltpu.VMEM),
        scratch_shapes=[shape(name) for name in names]
        + [shape(step) for step in messages]
        + [pltpu.SemaphoreType.DMA((len(messages),)), pltpu.SemaphoreType.DMA((len(messages),))]
        + [pltpu.SemaphoreType.REGULAR]
        + [
            pltpu.VMEM(populations.shape, populations.dtype),
            pltpu.VMEM(pore_mask.shape, pore_mask.dtype),
            pltpu.SemaphoreType.DMA((2,)),
        ],
        compiler_params=pltpu.CompilerParams(collective_id=0, has_side_effects=True),
    )(populations, pore_mask)


def solution(mesh):
    counts = tuple(mesh.shape[axis] for axis in ("gx", "gy", "gz"))
    placed = (P(None, "gx", "gy", "gz"), P("gx", "gy", "gz"))
    return jax.shard_map(
        functools.partial(body, counts),
        mesh=mesh,
        in_specs=placed,
        out_specs=P(None, "gx", "gy", "gz"),
        check_vma=False,
    )
```

```python
import functools

import jax
import jax.numpy as jnp
from jax import lax
from jax.experimental import pallas as pl
from jax.experimental.pallas import tpu as pltpu
from jax.sharding import PartitionSpec as P

MESH = pl.DeviceIdType.MESH

sound_sq = 2.0 / 3.0
relax_time = 0.8
pair_list = [(0, 0), (1, 1), (2, 2), (0, 1), (0, 2), (1, 2)]
triple_list = [
    (0, 0, 0),
    (1, 1, 1),
    (2, 2, 2),
    (0, 0, 1),
    (0, 0, 2),
    (1, 1, 0),
    (1, 1, 2),
    (2, 2, 0),
    (2, 2, 1),
    (0, 1, 2),
]
shell_weights = {
    (0, 0, 0): 1.0 / 12.0,
    (0, 0, 1): 1.0 / 12.0,
    (1, 1, 1): 1.0 / 27.0,
    (0, 0, 2): 2.0 / 135.0,
    (0, 2, 2): 1.0 / 432.0,
    (0, 0, 3): 1.0 / 1620.0,
}


def lattice():
    speeds = []
    weights = []
    for a in range(-3, 4):
        for b in range(-3, 4):
            for c in range(-3, 4):
                pattern = tuple(sorted((abs(a), abs(b), abs(c))))
                if pattern in shell_weights:
                    speeds.append((a, b, c))
                    weights.append(shell_weights[pattern])
    return speeds, weights


speeds, weights = lattice()
opposite = [speeds.index((-v[0], -v[1], -v[2])) for v in speeds]


def accumulate(total, factor, term):
    if factor == 0:
        return total
    if total is None:
        return term if factor == 1 else factor * term
    if factor == 1:
        return total + term
    if factor == -1:
        return total - term
    return total + factor * term


def collide(load, pore):
    rest = speeds.index((0, 0, 0))
    pairs = [(k, opposite[k]) for k in range(len(speeds)) if k > opposite[k]]
    density = weights[rest] * load(rest)
    first = [None] * 3
    second = {ab: None for ab in pair_list}
    third = {abc: None for abc in triple_list}
    for shell in shell_weights:
        members = [(k, o) for k, o in pairs if tuple(sorted(map(abs, speeds[k]))) == shell]
        if not members:
            continue
        part0, part1 = None, [None] * 3
        part2 = {ab: None for ab in pair_list}
        part3 = {abc: None for abc in triple_list}
        for k, o in members:
            v = speeds[k]
            even = load(k) + load(o)
            odd = load(k) - load(o)
            part0 = accumulate(part0, 1, even)
            for a, b in pair_list:
                part2[a, b] = accumulate(part2[a, b], v[a] * v[b], even)
            for a in range(3):
                part1[a] = accumulate(part1[a], v[a], odd)
            for a, b, c in triple_list:
                part3[a, b, c] = accumulate(part3[a, b, c], v[a] * v[b] * v[c], odd)
        w = shell_weights[shell]
        density = accumulate(density, w, part0)
        for a in range(3):
            first[a] = accumulate(first[a], w, part1[a])
        for ab in pair_list:
            if part2[ab] is not None:
                second[ab] = accumulate(second[ab], w, part2[ab])
        for abc in triple_list:
            if part3[abc] is not None:
                third[abc] = accumulate(third[abc], w, part3[abc])

    inverse = 1.0 / density
    u = [first[a] * inverse for a in range(3)]
    relax = 1.0 - 1.0 / relax_time
    const = density
    linear = [first[a] * (1.0 / sound_sq) for a in range(3)]
    quad, cubic = {}, {}
    flux = {}
    for a, b in pair_list:
        flux[a, b] = first[a] * u[b]
        moment = second[a, b]
        if a == b:
            moment = moment - sound_sq * density
        scale = (1.0 if a == b else 2.0) / (2.0 * sound_sq**2)
        quad[a, b] = (scale * (1.0 - relax)) * flux[a, b] + (scale * relax) * moment
        if a == b:
            const = const - sound_sq * quad[a, b]
    for a, b, c in triple_list:
        moment = third[a, b, c]
        if a == b == c:
            moment = moment - (3.0 * sound_sq) * first[a]
        elif a == b:
            moment = moment - sound_sq * first[c]
        pair = (a, b) if (a, b) in flux else (b, a)
        scale = {1: 1.0, 2: 3.0, 3: 6.0}[len({a, b, c})] / (6.0 * sound_sq**3)
        cubic[a, b, c] = (scale * (1.0 - relax)) * (flux[pair] * u[c]) + (scale * relax) * moment
        if a == b == c:
            linear[a] = linear[a] - (3.0 * sound_sq) * cubic[a, b, c]
        elif a == b:
            linear[c] = linear[c] - sound_sq * cubic[a, b, c]

    for k, o in sorted(pairs, key=lambda pair: speeds[pair[0]][0] == 0):
        v = speeds[k]
        even, odd = const, None
        for a, b in pair_list:
            even = accumulate(even, float(v[a] * v[b]), quad[a, b])
        for a in range(3):
            odd = accumulate(odd, float(v[a]), linear[a])
        for a, b, c in triple_list:
            odd = accumulate(odd, float(v[a] * v[b] * v[c]), cubic[a, b, c])
        yield k, jnp.where(pore, even + odd, load(o))
        yield o, jnp.where(pore, even - odd, load(k))
    yield rest, jnp.where(pore, const, load(rest))


def cut(speed, extent):
    if speed >= 0:
        return (0, extent - speed), (speed, extent), (extent - speed, extent), (0, speed)
    return (-speed, extent), (0, extent + speed), (0, -speed), (extent + speed, extent)


def merge_key(speed, rows, extent):
    return abs(speed) if 2 * rows <= extent else speed


def make_plan(nx, ny):
    sizes, slots, pieces = {}, {}, []
    for k, (cx, cy, cz) in enumerate(speeds):
        stay_from, stay_to, leave_from, leave_to = cut(cx, nx)
        own = []
        for source, land, dx in ((stay_from, stay_to, 0), (leave_from, leave_to, (cx > 0) - (cx < 0))):
            count = source[1] - source[0]
            if count == 0:
                continue
            where = {}
            for oy in (0, 1):
                for oz in (0, 1):
                    if (oy and not cy) or (oz and not cz) or (dx, oy, oz) == (0, 0, 0):
                        continue
                    key = (
                        dx,
                        oy,
                        oz,
                        cx,
                        merge_key(cy, abs(cy) if oy else ny - abs(cy), ny),
                        abs(cz) if oz else cz,
                    )
                    if key not in slots:
                        slots[key] = sizes.get((dx, oy, oz), 0)
                        sizes[dx, oy, oz] = slots[key] + count
                    where[oy, oz] = slots[key]
            own.append((source, land, dx, where))
        pieces.append(own)
    return sizes, pieces


def neighbours(count):
    return (1,) if count == 2 else (1, -1)


def step_kernel(counts, sizes, pieces, messages, names, pop_hbm, mask_hbm, out_ref, *scratch):
    nx, ny, nz = out_ref.shape[1:]
    *scratch, pop_ref, mask_ref, load_sem = scratch
    send = dict(zip(names, scratch[: len(names)]))
    recv = dict(zip(messages, scratch[len(names) : len(names) + len(messages)]))
    send_sem, recv_sem, ready = scratch[len(names) + len(messages) :]
    loads = [
        pltpu.make_async_copy(pop_hbm, pop_ref, load_sem.at[0]),
        pltpu.make_async_copy(mask_hbm, mask_ref, load_sem.at[1]),
    ]
    for load in loads:
        load.start()
    here = [lax.axis_index(axis) for axis in ("gx", "gy", "gz")]

    def target(step):
        return {
            axis: lax.rem(at + (s + count), count)
            for axis, at, s, count in zip(("gx", "gy", "gz"), here, step, counts)
            if s
        }

    barrier = pltpu.get_barrier_semaphore()
    for step in messages:
        if step[0] <= 0:
            pl.semaphore_signal(barrier, inc=1, device_id=target(step), device_id_type=MESH)

    for load in loads:
        load.wait()

    def block(span, rows, lanes):
        return (slice(*span), slice(*rows), slice(*lanes))

    copies = {}
    for number, step in enumerate(messages):
        kind = (step[0], abs(step[1]), abs(step[2]))
        copies[step] = pltpu.make_async_remote_copy(
            src_ref=send[kind],
            dst_ref=recv[step],
            send_sem=send_sem.at[number],
            recv_sem=recv_sem.at[number],
            device_id=target(step),
            device_id_type=MESH,
        )
    above = sum(step[0] > 0 for step in messages)

    pore = mask_ref[...] == 1
    every_lane = (0, nz)
    moving = sum(speed[0] != 0 for speed in speeds)
    for done, (k, plane) in enumerate(collide(lambda j: pop_ref[j], pore)):
        if done == moving:
            pl.semaphore_wait(barrier, len(messages) - above)
            for step in messages:
                if step[0] > 0:
                    copies[step].start()
            for step in messages:
                if step[0] > 0:
                    pl.semaphore_signal(ready, inc=1, device_id=target(step), device_id_type=MESH)
        cx, cy, cz = speeds[k]
        if cz:
            plane = pltpu.roll(plane, cz % nz, 2)
        y_stay, y_land, y_leave, y_wrap = cut(cy, ny)
        z_wrap = cut(cz, nz)[3]
        for source, land, dx, where in pieces[k]:
            count = source[1] - source[0]
            value = plane[slice(*source)]
            kept = value[:, slice(*y_stay)]
            if dx == 0:
                out_ref[(k,) + block(land, y_land, every_lane)] = kept
            else:
                at = where[0, 0]
                send[dx, 0, 0][block((at, at + count), y_land, every_lane)] = kept
            if cy:
                at = where[1, 0]
                moved = value[:, slice(*y_leave)]
                send[dx, 1, 0][block((at, at + count), y_wrap, every_lane)] = moved
            if cz:
                at = where[0, 1]
                send[dx, 0, 1][block((at, at + count), y_land, z_wrap)] = kept[:, :, slice(*z_wrap)]
            if cy and cz:
                at = where[1, 1]
                send[dx, 1, 1][block((at, at + count), y_wrap, z_wrap)] = moved[:, :, slice(*z_wrap)]

    for step in messages:
        if step[0] == 0:
            copies[step].start()
    pl.semaphore_wait(ready, above)
    for step in messages:
        if step[0] < 0:
            copies[step].start()

    def came_by(step, speed):
        return step == 0 or step * speed > 0

    for step in sorted(messages, key=lambda step: (0, -1, 1).index(step[0])):
        copies[step].wait_recv()
        got = recv[step]
        dx, sy, sz = step
        for k, (cx, cy, cz) in enumerate(speeds):
            if (sy and not cy) or (sz and not cz):
                continue
            if counts[1] != 2 and not came_by(sy, cy):
                continue
            if counts[2] != 2 and not came_by(sz, cz):
                continue
            _, y_land, _, y_wrap = cut(cy, ny)
            rows = y_wrap if sy else y_land
            lanes = cut(cz, nz)[3 if sz else 1]
            for source, land, piece_dx, where in pieces[k]:
                if piece_dx != dx:
                    continue
                at = where[abs(sy), abs(sz)]
                span = (at, at + source[1] - source[0])
                out_ref[(k,) + block(land, rows, lanes)] = got[block(span, rows, lanes)]
    for step in messages:
        copies[step].wait_send()


def body(counts, populations, pore_mask):
    nx, ny, nz = populations.shape[1:]
    sizes, pieces = make_plan(nx, ny)
    names = sorted(sizes)
    messages = []
    for dx, oy, oz in [(dx, oy, oz) for dx in (1, -1) for oz in (1, 0) for oy in (1, 0)] + [
        (0, 0, 1),
        (0, 1, 0),
        (0, 1, 1),
    ]:
        for sy in neighbours(counts[1]) if oy else (0,):
            for sz in neighbours(counts[2]) if oz else (0,):
                messages.append((dx, sy, sz))
    kernel = functools.partial(step_kernel, counts, sizes, pieces, messages, names)
    shape = lambda name: pltpu.VMEM((sizes[name[0], abs(name[1]), abs(name[2])], ny, nz), jnp.float32)
    return pl.pallas_call(
        kernel,
        out_shape=pltpu.VMEM(populations.shape, populations.dtype),
        in_specs=[pl.BlockSpec(memory_space=pl.ANY)] * 2,
        out_specs=pl.BlockSpec(memory_space=pltpu.VMEM),
        scratch_shapes=[shape(name) for name in names]
        + [shape(step) for step in messages]
        + [pltpu.SemaphoreType.DMA((len(messages),)), pltpu.SemaphoreType.DMA((len(messages),))]
        + [pltpu.SemaphoreType.REGULAR]
        + [
            pltpu.VMEM(populations.shape, populations.dtype),
            pltpu.VMEM(pore_mask.shape, pore_mask.dtype),
            pltpu.SemaphoreType.DMA((2,)),
        ],
        compiler_params=pltpu.CompilerParams(collective_id=0, has_side_effects=True),
    )(populations, pore_mask)


def solution(mesh):
    counts = tuple(mesh.shape[axis] for axis in ("gx", "gy", "gz"))
    placed = (P(None, "gx", "gy", "gz"), P("gx", "gy", "gz"))
    return jax.shard_map(
        functools.partial(body, counts),
        mesh=mesh,
        in_specs=placed,
        out_specs=P(None, "gx", "gy", "gz"),
        check_vma=False,
    )
```

```python
import functools

import jax
import jax.numpy as jnp
from jax import lax
from jax.experimental import pallas as pl
from jax.experimental.pallas import tpu as pltpu
from jax.sharding import PartitionSpec as P

MESH = pl.DeviceIdType.MESH

sound_sq = 2.0 / 3.0
relax_time = 0.8
pair_list = [(0, 0), (1, 1), (2, 2), (0, 1), (0, 2), (1, 2)]
triple_list = [
    (0, 0, 0),
    (1, 1, 1),
    (2, 2, 2),
    (0, 0, 1),
    (0, 0, 2),
    (1, 1, 0),
    (1, 1, 2),
    (2, 2, 0),
    (2, 2, 1),
    (0, 1, 2),
]
shell_weights = {
    (0, 0, 0): 1.0 / 12.0,
    (0, 0, 1): 1.0 / 12.0,
    (1, 1, 1): 1.0 / 27.0,
    (0, 0, 2): 2.0 / 135.0,
    (0, 2, 2): 1.0 / 432.0,
    (0, 0, 3): 1.0 / 1620.0,
}


def lattice():
    speeds = []
    weights = []
    for a in range(-3, 4):
        for b in range(-3, 4):
            for c in range(-3, 4):
                pattern = tuple(sorted((abs(a), abs(b), abs(c))))
                if pattern in shell_weights:
                    speeds.append((a, b, c))
                    weights.append(shell_weights[pattern])
    return speeds, weights


speeds, weights = lattice()
opposite = [speeds.index((-v[0], -v[1], -v[2])) for v in speeds]


def accumulate(total, factor, term):
    if factor == 0:
        return total
    if total is None:
        return term if factor == 1 else factor * term
    if factor == 1:
        return total + term
    if factor == -1:
        return total - term
    return total + factor * term


def collide(load, pore):
    rest = speeds.index((0, 0, 0))
    pairs = [(k, opposite[k]) for k in range(len(speeds)) if k > opposite[k]]
    density = weights[rest] * load(rest)
    first = [None] * 3
    second = {ab: None for ab in pair_list}
    third = {abc: None for abc in triple_list}
    for shell in shell_weights:
        members = [(k, o) for k, o in pairs if tuple(sorted(map(abs, speeds[k]))) == shell]
        if not members:
            continue
        part0, part1 = None, [None] * 3
        part2 = {ab: None for ab in pair_list}
        part3 = {abc: None for abc in triple_list}
        for k, o in members:
            v = speeds[k]
            even = load(k) + load(o)
            odd = load(k) - load(o)
            part0 = accumulate(part0, 1, even)
            for a, b in pair_list:
                part2[a, b] = accumulate(part2[a, b], v[a] * v[b], even)
            for a in range(3):
                part1[a] = accumulate(part1[a], v[a], odd)
            for a, b, c in triple_list:
                part3[a, b, c] = accumulate(part3[a, b, c], v[a] * v[b] * v[c], odd)
        w = shell_weights[shell]
        density = accumulate(density, w, part0)
        for a in range(3):
            first[a] = accumulate(first[a], w, part1[a])
        for ab in pair_list:
            if part2[ab] is not None:
                second[ab] = accumulate(second[ab], w, part2[ab])
        for abc in triple_list:
            if part3[abc] is not None:
                third[abc] = accumulate(third[abc], w, part3[abc])

    inverse = 1.0 / density
    u = [first[a] * inverse for a in range(3)]
    relax = 1.0 - 1.0 / relax_time
    const = density
    linear = [first[a] * (1.0 / sound_sq) for a in range(3)]
    quad, cubic = {}, {}
    flux = {}
    for a, b in pair_list:
        flux[a, b] = first[a] * u[b]
        moment = second[a, b]
        if a == b:
            moment = moment - sound_sq * density
        scale = (1.0 if a == b else 2.0) / (2.0 * sound_sq**2)
        quad[a, b] = (scale * (1.0 - relax)) * flux[a, b] + (scale * relax) * moment
        if a == b:
            const = const - sound_sq * quad[a, b]
    for a, b, c in triple_list:
        moment = third[a, b, c]
        if a == b == c:
            moment = moment - (3.0 * sound_sq) * first[a]
        elif a == b:
            moment = moment - sound_sq * first[c]
        pair = (a, b) if (a, b) in flux else (b, a)
        scale = {1: 1.0, 2: 3.0, 3: 6.0}[len({a, b, c})] / (6.0 * sound_sq**3)
        cubic[a, b, c] = (scale * (1.0 - relax)) * (flux[pair] * u[c]) + (scale * relax) * moment
        if a == b == c:
            linear[a] = linear[a] - (3.0 * sound_sq) * cubic[a, b, c]
        elif a == b:
            linear[c] = linear[c] - sound_sq * cubic[a, b, c]

    for k, o in sorted(pairs, key=lambda pair: speeds[pair[0]][0] == 0):
        v = speeds[k]
        even, odd = const, None
        for a, b in pair_list:
            even = accumulate(even, float(v[a] * v[b]), quad[a, b])
        for a in range(3):
            odd = accumulate(odd, float(v[a]), linear[a])
        for a, b, c in triple_list:
            odd = accumulate(odd, float(v[a] * v[b] * v[c]), cubic[a, b, c])
        yield k, jnp.where(pore, even + odd, load(o))
        yield o, jnp.where(pore, even - odd, load(k))
    yield rest, jnp.where(pore, const, load(rest))


def cut(speed, extent):
    if speed >= 0:
        return (0, extent - speed), (speed, extent), (extent - speed, extent), (0, speed)
    return (-speed, extent), (0, extent + speed), (0, -speed), (extent + speed, extent)


def merge_key(speed, rows, extent):
    return abs(speed) if 2 * rows <= extent else speed


def make_plan(nx, ny):
    sizes, slots, pieces = {}, {}, []
    for k, (cx, cy, cz) in enumerate(speeds):
        stay_from, stay_to, leave_from, leave_to = cut(cx, nx)
        own = []
        for source, land, dx in ((stay_from, stay_to, 0), (leave_from, leave_to, (cx > 0) - (cx < 0))):
            count = source[1] - source[0]
            if count == 0:
                continue
            where = {}
            for oy in (0, 1):
                for oz in (0, 1):
                    if (oy and not cy) or (oz and not cz) or (dx, oy, oz) == (0, 0, 0):
                        continue
                    key = (
                        dx,
                        oy,
                        oz,
                        cx,
                        merge_key(cy, abs(cy) if oy else ny - abs(cy), ny),
                        abs(cz) if oz else cz,
                    )
                    if key not in slots:
                        slots[key] = sizes.get((dx, oy, oz), 0)
                        sizes[dx, oy, oz] = slots[key] + count
                    where[oy, oz] = slots[key]
            own.append((source, land, dx, where))
        pieces.append(own)
    return sizes, pieces


def neighbours(count):
    return (1,) if count == 2 else (1, -1)


def step_kernel(counts, sizes, pieces, messages, names, pop_hbm, mask_hbm, out_ref, *scratch):
    nx, ny, nz = out_ref.shape[1:]
    *scratch, pop_ref, mask_ref, load_sem = scratch
    send = dict(zip(names, scratch[: len(names)]))
    recv = dict(zip(messages, scratch[len(names) : len(names) + len(messages)]))
    send_sem, recv_sem = scratch[len(names) + len(messages) :]
    loads = [
        pltpu.make_async_copy(pop_hbm, pop_ref, load_sem.at[0]),
        pltpu.make_async_copy(mask_hbm, mask_ref, load_sem.at[1]),
    ]
    for load in loads:
        load.start()
    here = [lax.axis_index(axis) for axis in ("gx", "gy", "gz")]

    def target(step):
        return {
            axis: lax.rem(at + (s + count), count)
            for axis, at, s, count in zip(("gx", "gy", "gz"), here, step, counts)
            if s
        }

    barrier = pltpu.get_barrier_semaphore()
    for step in messages:
        pl.semaphore_signal(barrier, inc=1, device_id=target(step), device_id_type=MESH)

    for load in loads:
        load.wait()

    def block(span, rows, lanes):
        return (slice(*span), slice(*rows), slice(*lanes))

    copies = {}
    for number, step in enumerate(messages):
        kind = (step[0], abs(step[1]), abs(step[2]))
        copies[step] = pltpu.make_async_remote_copy(
            src_ref=send[kind],
            dst_ref=recv[step],
            send_sem=send_sem.at[number],
            recv_sem=recv_sem.at[number],
            device_id=target(step),
            device_id_type=MESH,
        )

    pore = mask_ref[...] == 1
    every_lane = (0, nz)
    moving = sum(speed[0] != 0 for speed in speeds)
    for done, (k, plane) in enumerate(collide(lambda j: pop_ref[j], pore)):
        if done == moving:
            pl.semaphore_wait(barrier, len(messages))
            for step in messages:
                if step[0]:
                    copies[step].start()
        cx, cy, cz = speeds[k]
        if cz:
            plane = pltpu.roll(plane, cz % nz, 2)
        y_stay, y_land, y_leave, y_wrap = cut(cy, ny)
        z_wrap = cut(cz, nz)[3]
        for source, land, dx, where in pieces[k]:
            count = source[1] - source[0]
            value = plane[slice(*source)]
            kept = value[:, slice(*y_stay)]
            if dx == 0:
                out_ref[(k,) + block(land, y_land, every_lane)] = kept
            else:
                at = where[0, 0]
                send[dx, 0, 0][block((at, at + count), y_land, every_lane)] = kept
            if cy:
                at = where[1, 0]
                moved = value[:, slice(*y_leave)]
                send[dx, 1, 0][block((at, at + count), y_wrap, every_lane)] = moved
            if cz:
                at = where[0, 1]
                send[dx, 0, 1][block((at, at + count), y_land, z_wrap)] = kept[:, :, slice(*z_wrap)]
            if cy and cz:
                at = where[1, 1]
                send[dx, 1, 1][block((at, at + count), y_wrap, z_wrap)] = moved[:, :, slice(*z_wrap)]

    for step in messages:
        if step[0] == 0:
            copies[step].start()

    def came_by(step, speed):
        return step == 0 or step * speed > 0

    for step in sorted(messages, key=lambda step: (0, -1, 1).index(step[0])):
        copies[step].wait_recv()
        got = recv[step]
        dx, sy, sz = step
        for k, (cx, cy, cz) in enumerate(speeds):
            if (sy and not cy) or (sz and not cz):
                continue
            if counts[1] != 2 and not came_by(sy, cy):
                continue
            if counts[2] != 2 and not came_by(sz, cz):
                continue
            _, y_land, _, y_wrap = cut(cy, ny)
            rows = y_wrap if sy else y_land
            lanes = cut(cz, nz)[3 if sz else 1]
            for source, land, piece_dx, where in pieces[k]:
                if piece_dx != dx:
                    continue
                at = where[abs(sy), abs(sz)]
                span = (at, at + source[1] - source[0])
                out_ref[(k,) + block(land, rows, lanes)] = got[block(span, rows, lanes)]
    for step in messages:
        copies[step].wait_send()


def body(counts, populations, pore_mask):
    nx, ny, nz = populations.shape[1:]
    sizes, pieces = make_plan(nx, ny)
    names = sorted(sizes)
    messages = []
    for dx, oy, oz in [(dx, oy, oz) for dx in (1, -1) for oz in (1, 0) for oy in (1, 0)] + [
        (0, 0, 1),
        (0, 1, 0),
        (0, 1, 1),
    ]:
        for sy in neighbours(counts[1]) if oy else (0,):
            for sz in neighbours(counts[2]) if oz else (0,):
                messages.append((dx, sy, sz))
    kernel = functools.partial(step_kernel, counts, sizes, pieces, messages, names)
    shape = lambda name: pltpu.VMEM((sizes[name[0], abs(name[1]), abs(name[2])], ny, nz), jnp.float32)
    return pl.pallas_call(
        kernel,
        out_shape=pltpu.VMEM(populations.shape, populations.dtype),
        in_specs=[pl.BlockSpec(memory_space=pl.ANY)] * 2,
        out_specs=pl.BlockSpec(memory_space=pltpu.VMEM),
        scratch_shapes=[shape(name) for name in names]
        + [shape(step) for step in messages]
        + [pltpu.SemaphoreType.DMA((len(messages),)), pltpu.SemaphoreType.DMA((len(messages),))]
        + [
            pltpu.VMEM(populations.shape, populations.dtype),
            pltpu.VMEM(pore_mask.shape, pore_mask.dtype),
            pltpu.SemaphoreType.DMA((2,)),
        ],
        compiler_params=pltpu.CompilerParams(collective_id=0, has_side_effects=True),
    )(populations, pore_mask)


def solution(mesh):
    counts = tuple(mesh.shape[axis] for axis in ("gx", "gy", "gz"))
    placed = (P(None, "gx", "gy", "gz"), P("gx", "gy", "gz"))
    return jax.shard_map(
        functools.partial(body, counts),
        mesh=mesh,
        in_specs=placed,
        out_specs=P(None, "gx", "gy", "gz"),
        check_vma=False,
    )
```
